256 devices in a mesh: grp: 4 (over x_lo, core), blk: 64 (over y, z, x_hi).
Axes of the slice: x: 4 (x_hi: 2, x_lo: 2; x = x_hi * 2 + x_lo), y: 4, z: 8, core: 2. Of those that a mesh axis runs over, the one named last changes fastest.
Arguments:
- obs: bfloat16 [1572864, 256], P(('grp', 'blk')), may hold values from -6 to 6
- mask_bits: int32 [1572864, 32], P(('grp', 'blk')), may hold values from 0 to 255
- factors: bfloat16 [1572864, 256], P(('grp', 'blk')), may hold values from -0.375 to 0.375
- x_blocks: float32 [4, 256, 16384], P('grp', None, 'blk'), may hold values from -6 to 6
- first_moment: float32 [4, 256, 16384], P('grp', None, 'blk'), may hold values from -0.6 to 0.6
- second_moment: float32 [4, 256, 16384], P('grp', None, 'blk'), may hold values from 0.001 to 0.1
- ar_weights: float32 [25, 256], replicated, may hold values from -0.25 to 0.25
- stratum: int32 [1], replicated, may hold values from 0 to 63
Outputs:
- factors_next: bfloat16 [1572864, 256], P(('grp', 'blk'))
- x_next: float32 [4, 256, 16384], P('grp', None, 'blk')
- first_next: float32 [4, 256, 16384], P('grp', None, 'blk')
- second_next: float32 [4, 256, 16384], P('grp', None, 'blk')
The draws below stay inside these ranges and needn't reach their ends.
All inputs are finite; a program needn't handle non-finite values.
Results may differ from the reference program's by a relative error of at most 0.0013.
Values sent between devices are 32-bit elements; how exact they have to be, the bound alone decides.
A program may use at most 64 MiB of HBM per device.

```python
import math
import jax
import jax.numpy as jnp
from jax import lax

RANK = 256
SHORT = 24
SEASON = 168
TB = 256
SER_DEV = 6144
LAGS = 25
WORDS = 32
SERIES = 1572864
TIME = 16384
N_GRP = 4
N_BLK = 64


def with_ends(entries, key, low, high):
    extent = entries.shape
    spot = [jax.random.randint(jax.random.fold_in(key, axis), (), 0, extent[axis]) for axis in range(len(extent))]
    entries = entries.at[tuple(spot)].set(low)
    longest = extent.index(max(extent))
    spot[longest] = (spot[longest] + 1) % extent[longest]
    return entries.at[tuple(spot)].set(high)


def level_of(key, shape, pieces, least, top_value):
    def one(position, parts):
        draws = jax.random.uniform(jax.random.fold_in(jax.random.fold_in(key, 6), position), (parts,), jnp.float32, least / len(pieces), top_value / len(pieces))
        return jnp.repeat(jnp.exp(draws), shape[position] // parts).reshape((-1,) + (1,) * (len(shape) - position - 1))

    factor_of = one(*pieces[0])
    for cut in pieces[1:]:
        factor_of = factor_of * one(*cut)
    return factor_of


def bell_draw(own_key, dims, scale, reach, pieces=(), kind=jnp.bfloat16):
    values = jax.random.normal(own_key, dims, jnp.float32) * scale
    if len(pieces) > 0:
        values = level_of(own_key, dims, pieces, -0.22, 0.18) * values
    return jnp.clip(values, min=-reach, max=reach).astype(kind)


def setup_inputs(seed: int = 0) -> dict:
    key_list = jax.random.split(jax.random.key(seed), 9)
    obs = bell_draw(key_list[0], (SERIES, TB), 1.0, 6.0, ((0, 256),))
    mask_bits = with_ends(jax.random.randint(key_list[1], (SERIES, WORDS), 0, 256), jax.random.fold_in(key_list[1], 1), 0, 255).astype(jnp.int32)
    factors = bell_draw(key_list[2], (SERIES, RANK), RANK ** -0.5, 0.375, ((0, 256),))
    x_blocks = bell_draw(key_list[3], (N_GRP, RANK, TIME), 1.0, 6.0, ((0, 4), (2, 64)), jnp.float32)
    first_moment = bell_draw(key_list[4], (N_GRP, RANK, TIME), 0.1, 0.6, ((0, 4), (2, 64)), jnp.float32)
    second_moment = jnp.clip(jnp.exp(math.log(0.1) - 4.6051702 * jax.random.uniform(key_list[5], (N_GRP, RANK, TIME), jnp.float32) ** level_of(key_list[5], (N_GRP, RANK, TIME), ((0, 4), (2, 64)), -0.2, 0.2)), 0.001, 0.1)
    ar_weights = jnp.clip(jax.random.uniform(key_list[6], (LAGS, RANK), jnp.float32, -0.25, 0.25), -0.25, 0.25)
    stratum = jax.random.randint(key_list[7], (1,), 0, N_BLK).astype(jnp.int32)
    return dict(obs=obs, mask_bits=mask_bits, factors=factors, x_blocks=x_blocks, first_moment=first_moment, second_moment=second_moment, ar_weights=ar_weights, stratum=stratum)


beta_one = 0.9
beta_two = 0.999
adam_eps = 1e-08
step_rate = 0.05
factor_rate = 0.002
data_scale = 0.25

def unpack_mask(bits):
    shifts = jnp.arange(8, dtype=jnp.int32)
    flags = jnp.bitwise_and(jnp.right_shift(bits[:, :, None], shifts[None, None, :]), 1)
    return flags.reshape(bits.shape[0], bits.shape[1] * 8).astype(jnp.float32)

def local_update(obs_tile, bits, factor_tile, block, first, second, halo, ar_weights):
    width = block.shape[1]
    mask = unpack_mask(bits)
    block_half = block.astype(jnp.bfloat16)
    predicted = jnp.dot(factor_tile, block_half, preferred_element_type=jnp.float32)
    error = (mask * (predicted - obs_tile.astype(jnp.float32))).astype(jnp.bfloat16)
    grad_factor = lax.dot_general(error, block_half, (((1,), (1,)), ((), ())), preferred_element_type=jnp.float32)
    grad_data = lax.dot_general(factor_tile, error, (((0,), (0,)), ((), ())), preferred_element_type=jnp.float32)
    extended = jnp.concatenate([halo, block], axis=1)
    lag_list = list(range(1, SHORT + 1)) + [SEASON]
    fitted = jnp.zeros_like(block)
    for index, lag in enumerate(lag_list):
        fitted = fitted + ar_weights[index][:, None] * extended[:, SEASON - lag:SEASON - lag + width]
    resid = block - fitted
    backward = jnp.zeros_like(block)
    for index, lag in enumerate(lag_list):
        later = jnp.pad(resid[:, lag:], ((0, 0), (0, lag)))
        backward = backward + ar_weights[index][:, None] * later
    gradient = data_scale * grad_data + resid - backward
    first_new = beta_one * first + (1.0 - beta_one) * gradient
    second_new = beta_two * second + (1.0 - beta_two) * gradient * gradient
    block_new = block - step_rate * first_new / (jnp.sqrt(second_new) + adam_eps)
    factor_new = (factor_tile.astype(jnp.float32) - factor_rate * grad_factor).astype(jnp.bfloat16)
    return (factor_new, block_new, first_new, second_new)

def reference(obs, mask_bits, factors, x_blocks, first_moment, second_moment, ar_weights, stratum):
    groups = N_GRP
    blocks = N_BLK

    def split(arr):
        return arr.reshape(groups, RANK, blocks, TB).transpose(0, 2, 1, 3)
    x_split = split(x_blocks)
    m_split = split(first_moment)
    v_split = split(second_moment)
    halo_all = jnp.roll(x_split, 1, axis=1)[..., TB - SEASON:]
    slots = jnp.arange(blocks, dtype=jnp.int32)
    block_index = (slots + stratum[0]) % blocks
    keep = (block_index != 0).astype(jnp.float32)
    halo_all = halo_all * keep[None, :, None, None]
    obs_split = obs.reshape(groups * blocks, SER_DEV, TB)
    bits_split = mask_bits.reshape(groups * blocks, SER_DEV, TB // 8)
    fac_split = factors.reshape(groups * blocks, SER_DEV, RANK)

    def one_tile(tile):
        group = tile // blocks
        slot = tile % blocks
        return local_update(obs_split[tile], bits_split[tile], fac_split[tile], x_split[group, slot], m_split[group, slot], v_split[group, slot], halo_all[group, slot], ar_weights)
    fac_new, x_new, m_new, v_new = lax.map(one_tile, jnp.arange(groups * blocks, dtype=jnp.int32))

    def finish(arr):
        whole = arr.reshape(groups, blocks, RANK, TB)
        mean = lax.optimization_barrier(jnp.sum(whole, axis=0)) / groups
        turned = jnp.roll(mean, -1, axis=0)
        spread = jnp.broadcast_to(turned[None], (groups, blocks, RANK, TB))
        return spread.transpose(0, 2, 1, 3).reshape(groups, RANK, blocks * TB)
    return (fac_new.reshape(groups * blocks * SER_DEV, RANK), finish(x_new), finish(m_new), finish(v_new))
```

```python
import functools

import jax
import jax.numpy as jnp
from jax import lax
from jax.experimental import pallas as pl
from jax.experimental.pallas import tpu as pltpu
from jax.sharding import PartitionSpec as P

SHORT = 24
SEASON = 168
LAG_LIST = tuple(range(1, SHORT + 1)) + (SEASON,)

beta_one = 0.9
beta_two = 0.999
adam_eps = 1e-08
step_rate = 0.05
factor_rate = 0.002
data_scale = 0.25

MESH = pl.DeviceIdType.MESH
ROWS = 512
CHUNKS = 4


def kernel(
    n_blk,
    obs_hbm, mask_hbm, fac_hbm, x_hbm, m_hbm, v_hbm, war_hbm, stratum_ref,
    fnew, xout,
    both, mask, err, war_ref, block, first, second, zt, art, lhs, half_t, grad_t,
    share, got_one, held_two, sent_two, got_two, sent_three,
    load_sem, mask_sem, small_sem, halo_sem, sem_one, sem_two, sem_three, sem_four, sem_five, sem_six,
):
    series = obs_hbm.shape[0]
    rank = obs_hbm.shape[1]
    width = x_hbm.shape[2]
    rows = min(ROWS, series)
    tiles = series // rows
    piece = rank // 4 // CHUNKS
    grp = lax.axis_index("grp")
    blk = lax.axis_index("blk")
    core = lax.rem(grp, 2)
    near = lax.div(grp, 2)
    partner = (near * 2 + 1 - core, blk)
    across = ((1 - near) * 2 + core, blk)
    before = lax.rem(blk + n_blk - 1, n_blk)
    after = lax.rem(blk + 1, n_blk)
    down = ((1 - near) * 2 + core, before)
    up = ((1 - near) * 2 + core, after)
    halo_to = (grp, after)
    halo_from = (grp, before)

    barrier = pltpu.get_barrier_semaphore()
    for other in (partner, across, down, up, halo_to, halo_from):
        pl.semaphore_signal(barrier, inc=1, device_id=other, device_id_type=MESH)

    small = [
        pltpu.make_async_copy(x_hbm.at[0], block, small_sem.at[0]),
        pltpu.make_async_copy(m_hbm.at[0], first, small_sem.at[1]),
        pltpu.make_async_copy(v_hbm.at[0], second, small_sem.at[2]),
        pltpu.make_async_copy(war_hbm, war_ref, small_sem.at[3]),
    ]
    small[0].start()
    mask_copy = pltpu.make_async_copy(mask_hbm, mask, mask_sem)
    mask_copy.start()

    def loads(index):
        span = pl.ds(pl.multiple_of(index * rows, rows), rows)
        return (
            pltpu.make_async_copy(fac_hbm.at[span], both.at[span, pl.ds(0, rank)], load_sem.at[0, index]),
            pltpu.make_async_copy(obs_hbm.at[span], both.at[span, pl.ds(rank, width)], load_sem.at[1, index]),
        )

    def start_loads(index, carry):
        for copy in loads(index):
            copy.start()
        return carry

    lax.fori_loop(0, tiles, start_loads, 0)
    for copy in small[1:]:
        copy.start()

    small[0].wait()
    block_t = block[...].T
    zt[pl.ds(SEASON, width), :] = block_t
    half = block_t.astype(jnp.bfloat16)
    half_t[...] = half
    lhs[:, pl.ds(0, rank)] = half
    row_id = lax.broadcasted_iota(jnp.int32, (width, width), 0)
    col_id = lax.broadcasted_iota(jnp.int32, (width, width), 1)
    lhs[:, pl.ds(rank, width)] = jnp.where(row_id == col_id, -1.0, 0.0).astype(jnp.bfloat16)
    grad_t[...] = jnp.zeros_like(grad_t)

    pl.semaphore_wait(barrier, 6)
    halo = pltpu.make_async_remote_copy(
        src_ref=zt.at[pl.ds(width, SEASON)],
        dst_ref=zt.at[pl.ds(0, SEASON)],
        send_sem=halo_sem.at[0],
        recv_sem=halo_sem.at[1],
        device_id=halo_to,
        device_id_type=MESH,
    )
    halo.start()
    mask_copy.wait()

    bit = jnp.left_shift(1, lax.broadcasted_iota(jnp.int32, (1, 8, 1), 1))

    def one_tile(index, carry):
        span = pl.ds(pl.multiple_of(index * rows, rows), rows)
        for copy in loads(index):
            copy.wait()
        part = both[span, :]
        diff = lax.dot_general(
            lhs[...], part, (((1,), (1,)), ((), ())), preferred_element_type=jnp.float32
        )
        words = mask[:, span]
        seen = jnp.bitwise_and(words[:, None, :], bit) != 0
        diff = jnp.where(seen, diff.reshape(width // 8, 8, rows), 0.0).reshape(width, rows)
        rounded = diff.astype(jnp.bfloat16)
        err[:, span] = rounded
        grad_t[...] += lax.dot_general(
            rounded, part[:, :rank], (((1,), (0,)), ((), ())), preferred_element_type=jnp.float32
        )
        return carry

    lax.fori_loop(0, tiles, one_tile, 0)

    small[3].wait()
    halo.wait_recv()
    keep = jnp.where(lax.rem(blk + stratum_ref[0], n_blk) == 0, 0.0, 1.0)
    zt[pl.ds(0, SEASON), :] = zt[pl.ds(0, SEASON), :] * keep
    step = 64
    for start in range(0, width, step):
        fitted = jnp.zeros((step, rank), jnp.float32)
        for index, lag in enumerate(LAG_LIST):
            fitted = fitted + war_ref[pl.ds(index, 1), :] * zt[pl.ds(SEASON + start - lag, step), :]
        art[pl.ds(start, step), :] = zt[pl.ds(SEASON + start, step), :] - fitted
    art[pl.ds(width, SEASON), :] = jnp.zeros((SEASON, rank), jnp.float32)
    for start in range(0, width, step):
        backward = jnp.zeros((step, rank), jnp.float32)
        for index, lag in enumerate(LAG_LIST):
            if start + lag < width:
                backward = backward + war_ref[pl.ds(index, 1), :] * art[pl.ds(start + lag, step), :]
        spot = pl.ds(start, step)
        grad_t[spot, :] = data_scale * grad_t[spot, :] + art[spot, :] - backward

    small[1].wait()
    small[2].wait()
    gradient = grad_t[...].T
    first_new = beta_one * first[...] + (1.0 - beta_one) * gradient
    second_new = beta_two * second[...] + (1.0 - beta_two) * gradient * gradient
    block_new = block[...] - step_rate * first_new / (jnp.sqrt(second_new) + adam_eps)
    shape = (2, 2, rank // 4, width)
    share[0] = block_new.reshape(shape)
    share[1] = first_new.reshape(shape)
    share[2] = second_new.reshape(shape)

    def factors_tile(index):
        span = pl.ds(pl.multiple_of(index * rows, rows), rows)
        grad = lax.dot_general(
            err[:, span], half_t[...], (((0,), (0,)), ((), ())), preferred_element_type=jnp.float32
        )
        old = both[span, pl.ds(0, rank)].astype(jnp.float32)
        fnew[span, :] = (old - factor_rate * grad).astype(jnp.bfloat16)

    def factors_span(low, high):
        def one(index, carry):
            factors_tile(index)
            return carry

        lax.fori_loop(low, high, one, 0)

    def spot(k):
        return pl.ds(k * piece, piece)

    def remote(src, dst, sem, k, to):
        return pltpu.make_async_remote_copy(
            src_ref=src, dst_ref=dst, send_sem=sem.at[0, k], recv_sem=sem.at[1, k],
            device_id=to, device_id_type=MESH,
        )

    hop_one = [remote(share.at[:, 1 - core, :, spot(k)], got_one.at[k], sem_one, k, partner) for k in range(CHUNKS)]
    hop_two = [remote(sent_two.at[k], got_two.at[k], sem_two, k, across) for k in range(CHUNKS)]
    hop_three = [
        remote(sent_three.at[k], xout.at[:, core, near, spot(k)], sem_three, k, down) for k in range(CHUNKS)
    ]
    landed = [xout.at[:, core, 1 - near, spot(k)] for k in range(CHUNKS)]
    hop_four = [remote(landed[k], landed[k], sem_four, k, across) for k in range(CHUNKS)]
    hop_five = [remote(landed[k], landed[k], sem_five, k, partner) for k in range(CHUNKS)]
    crossed = [xout.at[:, core, near, spot(k)] for k in range(CHUNKS)]
    hop_six = [remote(crossed[k], crossed[k], sem_six, k, partner) for k in range(CHUNKS)]

    cuts = [tiles * i // 3 for i in range(4)]
    for k in range(CHUNKS):
        hop_one[k].start()
    factors_span(cuts[0], cuts[1])
    for k in range(CHUNKS):
        hop_one[k].wait_recv()
        sent_two[k] = share[:, core, 1 - near, spot(k)] + got_one[k, :, 1 - near]
        held_two[k] = share[:, core, near, spot(k)] + got_one[k, :, near]
        hop_two[k].start()
    factors_span(cuts[1], cuts[2])
    for k in range(CHUNKS):
        hop_two[k].wait_recv()
        sent_three[k] = (held_two[k] + got_two[k]) * 0.25
        hop_three[k].start()
    factors_span(cuts[2], cuts[3])
    for k in range(CHUNKS):
        hop_three[k].wait_recv()
        hop_four[k].start()
        hop_five[k].start()
    for k in range(CHUNKS):
        hop_four[k].wait_recv()
        hop_six[k].start()
    for k in range(CHUNKS):
        hop_five[k].wait_recv()
        hop_six[k].wait_recv()
    halo.wait_send()
    for hop in (hop_one, hop_two, hop_three, hop_four, hop_five, hop_six):
        for k in range(CHUNKS):
            hop[k].wait_send()


def body(obs, mask_bits, factors, x_blocks, first_moment, second_moment, ar_weights, stratum):
    series, rank = factors.shape
    width = obs.shape[1]
    words = mask_bits.shape[1]
    rows = min(ROWS, series)
    tiles = series // rows
    piece = rank // 4 // CHUNKS
    n_blk = lax.axis_size("blk")
    in_hbm = pl.BlockSpec(memory_space=pltpu.HBM)
    in_vmem = pl.BlockSpec(memory_space=pltpu.VMEM)
    f32, bf16 = jnp.float32, jnp.bfloat16
    dma = pltpu.SemaphoreType.DMA
    factor_new, turned = pl.pallas_call(
        functools.partial(kernel, n_blk),
        out_shape=(
            jax.ShapeDtypeStruct((series, rank), bf16),
            jax.ShapeDtypeStruct((3, 2, 2, rank // 4, width), f32),
        ),
        in_specs=[in_hbm] * 7 + [pl.BlockSpec(memory_space=pltpu.SMEM)],
        out_specs=(in_vmem, in_vmem),
        scratch_shapes=[
            pltpu.VMEM((series, rank + width), bf16),
            pltpu.VMEM((words, series), jnp.int32),
            pltpu.VMEM((width, series), bf16),
            pltpu.VMEM((len(LAG_LIST), rank), f32),
            pltpu.VMEM((rank, width), f32),
            pltpu.VMEM((rank, width), f32),
            pltpu.VMEM((rank, width), f32),
            pltpu.VMEM((SEASON + width, rank), f32),
            pltpu.VMEM((width + SEASON, rank), f32),
            pltpu.VMEM((width, rank + width), bf16),
            pltpu.VMEM((width, rank), bf16),
            pltpu.VMEM((width, rank), f32),
            pltpu.VMEM((3, 2, 2, rank // 4, width), f32),
            pltpu.VMEM((CHUNKS, 3, 2, piece, width), f32),
            pltpu.VMEM((CHUNKS, 3, piece, width), f32),
            pltpu.VMEM((CHUNKS, 3, piece, width), f32),
            pltpu.VMEM((CHUNKS, 3, piece, width), f32),
            pltpu.VMEM((CHUNKS, 3, piece, width), f32),
            dma((2, tiles)),
            dma,
            dma((4,)),
            dma((2,)),
        ]
        + [dma((2, CHUNKS))] * 6,
        compiler_params=pltpu.CompilerParams(
            collective_id=0, has_side_effects=True, vmem_limit_bytes=48 * 1024 * 1024
        ),
        name="stratum_step",
    )(
        *[
            pltpu.with_memory_space_constraint(value, pltpu.HBM)
            for value in (obs, mask_bits.T, factors, x_blocks, first_moment, second_moment, ar_weights)
        ],
        stratum,
    )
    turned = turned.reshape(3, 1, rank, width)
    return (factor_new, turned[0], turned[1], turned[2])


def solution(mesh):
    placed = (
        P(("grp", "blk"), None),
        P(("grp", "blk"), None),
        P(("grp", "blk"), None),
        P("grp", None, "blk"),
        P("grp", None, "blk"),
        P("grp", None, "blk"),
        P(),
        P(),
    )
    return jax.shard_map(
        body,
        mesh=mesh,
        in_specs=placed,
        out_specs=(
            P(("grp", "blk"), None),
            P("grp", None, "blk"),
            P("grp", None, "blk"),
            P("grp", None, "blk"),
        ),
        check_vma=False,
    )
```

```python
import functools

import jax
import jax.numpy as jnp
from jax import lax
from jax.experimental import pallas as pl
from jax.experimental.pallas import tpu as pltpu
from jax.sharding import PartitionSpec as P

SHORT = 24
SEASON = 168
LAGS = SHORT + 1

beta_one = 0.9
beta_two = 0.999
adam_eps = 1e-08
step_rate = 0.05
factor_rate = 0.002
data_scale = 0.25

MESH = pl.DeviceIdType.MESH
TILES = ((0, 1024), (1024, 1536), (2560, 1536), (4096, 2048))
SIDE = ((128, 40), (0, 40))
AHEAD = ((40, 48), (88, 40))
HALF = 128
PARTS = 2
BLOCK = 64
STORES = 8


def kernel(
    n_blk,
    obs_hbm, mask_hbm, fac_hbm, x_hbm, m_hbm, v_hbm, war_hbm, stratum,
    fnew, xout,
    obs, mask, fac, err, war, block, first, second, zt, art, pt, half_t, grad,
    side_stop, ahead_stop, share, got_one, held_two, sent_two, got_two, sent_three,
    load_sem, small_sem, side_sem, ahead_sem, sem_one, sem_two, sem_three, sem_four, sem_five, sem_six,
):
    rank = obs_hbm.shape[1]
    width = x_hbm.shape[2]
    quarter = rank // 4
    piece = quarter // PARTS
    grp = lax.axis_index("grp")
    blk = lax.axis_index("blk")
    core = lax.rem(grp, 2)
    near = lax.div(grp, 2)
    far = 1 - near
    partner = (near * 2 + 1 - core, blk)
    across = (far * 2 + core, blk)
    down = (far * 2 + core, lax.rem(blk + n_blk - 1, n_blk))
    up = (far * 2 + core, lax.rem(blk + 1, n_blk))

    small = [
        pltpu.make_async_copy(x_hbm.at[0], block, small_sem.at[0]),
        pltpu.make_async_copy(war_hbm, war, small_sem.at[1]),
        pltpu.make_async_copy(m_hbm.at[0], first, small_sem.at[2]),
        pltpu.make_async_copy(v_hbm.at[0], second, small_sem.at[3]),
    ]
    small[0].start()
    loads = []
    for index, (low, rows) in enumerate(TILES):
        span = pl.ds(low, rows)
        loads.append(
            [
                pltpu.make_async_copy(fac_hbm.at[span], fac.at[span], load_sem.at[0, index]),
                pltpu.make_async_copy(mask_hbm.at[:, span], mask.at[:, span], load_sem.at[1, index]),
                pltpu.make_async_copy(obs_hbm.at[span], obs.at[span], load_sem.at[2, index]),
            ]
        )
    for copy in loads[0]:
        copy.start()

    barrier = pltpu.get_barrier_semaphore()
    for other in (partner, across, down):
        pl.semaphore_signal(barrier, inc=1, device_id=other, device_id_type=MESH)
    for copies in loads[1:]:
        for copy in copies:
            copy.start()
    for copy in small[1:]:
        copy.start()

    small[0].wait()
    block_t = block[...].T
    zt[pl.ds(SEASON, width), :] = block_t
    half = block[...].astype(jnp.bfloat16)
    half_t[...] = block_t.astype(jnp.bfloat16)
    grad[...] = jnp.zeros_like(grad)
    art[pl.ds(width, BLOCK), :] = jnp.zeros((BLOCK, rank), jnp.float32)
    spread_row = lax.broadcasted_iota(jnp.int32, (width // 8, width), 0)
    spread_col = lax.broadcasted_iota(jnp.int32, (width // 8, width), 1)
    spread = jnp.where(jnp.right_shift(spread_col, 3) == spread_row, 1.0, 0.0).astype(jnp.bfloat16)
    bit = jnp.left_shift(1, jnp.bitwise_and(lax.broadcasted_iota(jnp.int32, (1, width), 1), 7))

    def remote(src, dst, sem, k, to):
        return pltpu.make_async_remote_copy(
            src_ref=src, dst_ref=dst, send_sem=sem.at[0, k], recv_sem=sem.at[1, k],
            device_id=to, device_id_type=MESH,
        )

    side_one, side_two, ahead_one, ahead_two = [], [], [], []
    for k, (low, rows) in enumerate(SIDE):
        stop = side_stop.at[k, pl.ds(0, rows)]
        side_one.append(remote(zt.at[pl.ds(width + low, rows)], stop, side_sem, k, across))
        side_two.append(remote(stop, zt.at[pl.ds(low, rows)], side_sem, 2 + k, up))
    for k, (low, rows) in enumerate(AHEAD):
        stop = ahead_stop.at[k, pl.ds(0, rows)]
        ahead_one.append(remote(zt.at[pl.ds(width + low, rows)], stop, ahead_sem, k, up))
        ahead_two.append(remote(stop, zt.at[pl.ds(low, rows)], ahead_sem, 2 + k, across))

    pl.semaphore_wait(barrier, 3)
    for k in range(2):
        side_one[k].start()
        ahead_one[k].start()

    def error_tile(index):
        low, rows = TILES[index]
        span = pl.ds(low, rows)
        for copy in loads[index]:
            copy.wait()
        part = fac[span, :]
        diff = jnp.dot(part, half, preferred_element_type=jnp.float32) - obs[span, :].astype(jnp.float32)
        words = mask[:, span].astype(jnp.float32).astype(jnp.bfloat16)
        wide = lax.dot_general(words, spread, (((0,), (0,)), ((), ())), preferred_element_type=jnp.float32)
        seen = jnp.bitwise_and(wide.astype(jnp.int32), bit) != 0
        rounded = jnp.where(seen, diff, 0.0).astype(jnp.bfloat16)
        err[span, :] = rounded
        grad[...] += lax.dot_general(
            part, rounded, (((0,), (0,)), ((), ())), preferred_element_type=jnp.float32
        )

    def factors_span(low, rows):
        span = pl.ds(low, rows)
        step = jnp.dot(err[span, :], half_t[...], preferred_element_type=jnp.float32)
        fnew[span, :] = (fac[span, :].astype(jnp.float32) - factor_rate * step).astype(jnp.bfloat16)

    def weight(lag_index, lanes):
        return war[pl.ds(lag_index, 1), lanes]

    def residual(start, lanes):
        near_rows = zt[pl.ds(SEASON - SHORT + start, BLOCK + SHORT), lanes]
        fitted = weight(SHORT, lanes) * zt[pl.ds(start, BLOCK), lanes]
        for turn in range(8):
            moved = near_rows if turn == 0 else pltpu.roll(near_rows, turn, 0)
            for tile in range(4):
                lag = 8 * tile + turn
                if 1 <= lag <= SHORT:
                    low = SHORT - 8 * tile
                    fitted = fitted + weight(lag - 1, lanes) * moved[low : low + BLOCK]
        art[pl.ds(start, BLOCK), lanes] = near_rows[SHORT:] - fitted

    def prior_gradient(start, lanes):
        rows = art[pl.ds(start, BLOCK + SHORT), lanes]
        total = rows[:BLOCK]
        for turn in range(8):
            moved = rows if turn == 0 else pltpu.roll(rows, BLOCK + SHORT - turn, 0)
            for tile in range(4):
                lag = 8 * tile + turn
                if 1 <= lag <= SHORT:
                    total = total - weight(lag - 1, lanes) * moved[8 * tile : 8 * tile + BLOCK]
        if start + SEASON < width:
            total = total - weight(SHORT, lanes) * art[pl.ds(start + SEASON, BLOCK), lanes]
        pt[pl.ds(start, BLOCK), lanes] = total

    all_lanes = [pl.ds(at, 128) for at in range(0, rank, 128)]

    def update(which):
        starts = [which * HALF + at for at in range(0, HALF, BLOCK)]
        for start in starts:
            for lanes in all_lanes:
                residual(start, lanes)
        for start in starts:
            for lanes in all_lanes:
                prior_gradient(start, lanes)
        cols = pl.ds(which * HALF, HALF)
        gradient = data_scale * grad[:, cols] + pt[cols, :].T
        first_new = beta_one * first[:, cols] + (1.0 - beta_one) * gradient
        second_new = beta_two * second[:, cols] + (1.0 - beta_two) * gradient * gradient
        block_new = block[:, cols] - step_rate * first_new / (jnp.sqrt(second_new) + adam_eps)
        shape = (2, 2, quarter, HALF)
        share[which, 0] = block_new.reshape(shape)
        share[which, 1] = first_new.reshape(shape)
        share[which, 2] = second_new.reshape(shape)

    chunks = [(which, pl.ds(p * piece, piece)) for which in (1, 0) for p in range(PARTS)]
    hop_one, hop_two, hop_three, hop_four, hop_five, hop_six = [], [], [], [], [], []
    for k, (which, ranks) in enumerate(chunks):
        landed = xout.at[which, :, core, far, ranks]
        crossed = xout.at[which, :, core, near, ranks]
        hop_one.append(remote(share.at[which, :, 1 - core, :, ranks], got_one.at[k], sem_one, k, partner))
        hop_two.append(remote(sent_two.at[k], got_two.at[k], sem_two, k, across))
        hop_three.append(remote(sent_three.at[k], crossed, sem_three, k, down))
        hop_four.append(remote(landed, landed, sem_four, k, across))
        hop_five.append(remote(landed, landed, sem_five, k, partner))
        hop_six.append(remote(crossed, crossed, sem_six, k, partner))

    def fold_core(k):
        which, ranks = chunks[k]
        hop_one[k].wait_recv()
        sent_two[k] = share[which, :, core, far, ranks] + got_one[k, :, far]
        hop_two[k].start()
        held_two[k] = share[which, :, core, near, ranks] + got_one[k, :, near]

    def fold_chip(k):
        hop_two[k].wait_recv()
        sent_three[k] = (held_two[k] + got_two[k]) * 0.25
        hop_three[k].start()

    def spread_landed(k):
        hop_three[k].wait_recv()
        hop_four[k].start()
        hop_five[k].start()

    def spread_crossed(k):
        hop_four[k].wait_recv()
        hop_six[k].start()

    error_tile(0)
    error_tile(1)
    for k in range(2):
        side_one[k].wait_recv()
        side_two[k].start()
    error_tile(2)
    error_tile(3)
    for k in range(2):
        ahead_one[k].wait_recv()
        ahead_two[k].start()

    for copy in small[1:]:
        copy.wait()
    keep = jnp.where(lax.rem(blk + stratum[0], n_blk) == 0, 0.0, 1.0)
    side_two[0].wait_recv()
    late = pl.ds(SIDE[0][0], SIDE[0][1])
    zt[late, :] = zt[late, :] * keep
    update(1)
    hop_one[0].start()
    hop_one[1].start()
    factors_span(0, 1024)
    fold_core(0)
    fold_core(1)
    side_two[1].wait_recv()
    for k in range(2):
        ahead_two[k].wait_recv()
    early = pl.ds(0, SIDE[0][0])
    zt[early, :] = zt[early, :] * keep
    update(0)
    hop_one[2].start()
    hop_one[3].start()
    factors_span(1024, 1024)
    fold_core(2)
    fold_core(3)
    fold_chip(0)
    fold_chip(1)
    factors_span(2048, 2048)
    fold_chip(2)
    spread_landed(0)
    fold_chip(3)
    spread_landed(1)
    factors_span(4096, 2048)
    spread_landed(2)
    spread_crossed(0)
    spread_landed(3)
    spread_crossed(1)
    spread_crossed(2)
    spread_crossed(3)
    for k in range(2 * PARTS):
        hop_five[k].wait_recv()
        hop_six[k].wait_recv()
    for copies in (side_one, side_two, ahead_one, ahead_two):
        for copy in copies:
            copy.wait_send()
    for hop in (hop_one, hop_two, hop_three, hop_four, hop_five, hop_six):
        for copy in hop:
            copy.wait_send()


def store_kernel(fnew, xout, fac_out, x_out, m_out, v_out, sem):
    width = x_out.shape[2]
    copies = []
    step = fnew.shape[0] // STORES
    for index in range(STORES):
        span = pl.ds(index * step, step)
        copies.append(pltpu.make_async_copy(fnew.at[span], fac_out.at[span], sem.at[index]))
    for index, out in enumerate((x_out, m_out, v_out)):
        for which in range(width // HALF):
            copies.append(
                pltpu.make_async_copy(
                    xout.at[which, index], out.at[0, :, pl.ds(which * HALF, HALF)], sem.at[STORES + 2 * index + which]
                )
            )
    for copy in copies:
        copy.start()
    for copy in copies:
        copy.wait()


def body(obs, mask_bits, factors, x_blocks, first_moment, second_moment, ar_weights, stratum):
    series, rank = factors.shape
    width = obs.shape[1]
    words = mask_bits.shape[1]
    quarter = rank // 4
    piece = quarter // PARTS
    chunks = 2 * PARTS
    n_blk = lax.axis_size("blk")
    in_hbm = pl.BlockSpec(memory_space=pltpu.HBM)
    in_vmem = pl.BlockSpec(memory_space=pltpu.VMEM)
    f32, bf16 = jnp.float32, jnp.bfloat16
    dma = pltpu.SemaphoreType.DMA
    factor_new, turned = pl.pallas_call(
        functools.partial(kernel, n_blk),
        out_shape=(
            jax.ShapeDtypeStruct((series, rank), bf16),
            jax.ShapeDtypeStruct((2, 3, 2, 2, quarter, HALF), f32),
        ),
        in_specs=[in_hbm] * 7 + [pl.BlockSpec(memory_space=pltpu.SMEM)],
        out_specs=(in_vmem, in_vmem),
        scratch_shapes=[
            pltpu.VMEM((series, width), bf16),
            pltpu.VMEM((words, series), jnp.int32),
            pltpu.VMEM((series, rank), bf16),
            pltpu.VMEM((series, width), bf16),
            pltpu.VMEM((LAGS, rank), f32),
            pltpu.VMEM((rank, width), f32),
            pltpu.VMEM((rank, width), f32),
            pltpu.VMEM((rank, width), f32),
            pltpu.VMEM((SEASON + width, rank), f32),
            pltpu.VMEM((width + BLOCK, rank), f32),
            pltpu.VMEM((width, rank), f32),
            pltpu.VMEM((width, rank), bf16),
            pltpu.VMEM((rank, width), f32),
            pltpu.VMEM((2, 48, rank), f32),
            pltpu.VMEM((2, 48, rank), f32),
            pltpu.VMEM((2, 3, 2, 2, quarter, HALF), f32),
            pltpu.VMEM((chunks, 3, 2, piece, HALF), f32),
            pltpu.VMEM((chunks, 3, piece, HALF), f32),
            pltpu.VMEM((chunks, 3, piece, HALF), f32),
            pltpu.VMEM((chunks, 3, piece, HALF), f32),
            pltpu.VMEM((chunks, 3, piece, HALF), f32),
            dma((3, len(TILES))),
            dma((4,)),
            dma((2, 4)),
            dma((2, 4)),
        ]
        + [dma((2, chunks))] * 6,
        compiler_params=pltpu.CompilerParams(
            collective_id=0, has_side_effects=True, vmem_limit_bytes=48 * 1024 * 1024
        ),
        name="stratum_step",
    )(
        *[
            pltpu.with_memory_space_constraint(value, pltpu.HBM)
            for value in (obs, mask_bits.T, factors, x_blocks, first_moment, second_moment, ar_weights)
        ],
        stratum,
    )
    turned = turned.reshape(2, 3, rank, HALF)
    return STORE(factor_new, turned, series, rank, width)


def store_plain(factor_new, turned, series, rank, width):
    whole = jnp.concatenate([turned[0], turned[1]], axis=2)
    return (factor_new, whole[0][None], whole[1][None], whole[2][None])


def store_by_kernel(factor_new, turned, series, rank, width):
    f32, bf16 = jnp.float32, jnp.bfloat16
    in_vmem = pl.BlockSpec(memory_space=pltpu.VMEM)
    in_hbm = pl.BlockSpec(memory_space=pltpu.HBM)
    out = jax.ShapeDtypeStruct((1, rank, width), f32)
    return tuple(
        pl.pallas_call(
            store_kernel,
            out_shape=(jax.ShapeDtypeStruct((series, rank), bf16), out, out, out),
            in_specs=[in_vmem] * 2,
            out_specs=[in_hbm] * 4,
            scratch_shapes=[pltpu.SemaphoreType.DMA((STORES + 6,))],
            compiler_params=pltpu.CompilerParams(vmem_limit_bytes=8 * 1024 * 1024),
            name="store_outputs",
        )(factor_new, turned)
    )


STORE = store_by_kernel


def solution(mesh):
    placed = (
        P(("grp", "blk"), None),
        P(("grp", "blk"), None),
        P(("grp", "blk"), None),
        P("grp", None, "blk"),
        P("grp", None, "blk"),
        P("grp", None, "blk"),
        P(),
        P(),
    )
    return jax.shard_map(
        body,
        mesh=mesh,
        in_specs=placed,
        out_specs=(
            P(("grp", "blk"), None),
            P("grp", None, "blk"),
            P("grp", None, "blk"),
            P("grp", None, "blk"),
        ),
        check_vma=False,
    )
```
